32 devices in a mesh: gz: 8 (over z, y), gy: 4 (over x, core).
Axes of the slice: x: 2, y: 2, z: 4, core: 2. Of those that a mesh axis runs over, the one named last changes fastest.
Arguments:
- noisy_field: bfloat16 [32, 16, 256, 256], P(None, 'gz', 'gy'), may hold values from -6 to 6
- spectral_weights: bfloat16 [2, 2, 6912, 32, 32], P(None, None, 'gz', None, 'gy'), may hold values from -0.75 to 0.75
- skip_weights: bfloat16 [2, 32, 32], replicated, may hold values from -1 to 1
- in_weights: bfloat16 [2, 256, 32], replicated, may hold values from -1 to 1
- in_bias: float32 [2, 256], replicated, may hold values from -3 to 3
- out_weights: bfloat16 [2, 32, 256], replicated, may hold values from -0.375 to 0.375
Outputs:
- refined: bfloat16 [32, 16, 256, 256], P(None, 'gz', 'gy')
The draws below stay inside these ranges and needn't reach their ends.
All inputs are finite; a program needn't handle non-finite values.
Results may differ from the reference program's by a relative error of at most 0.023.
Values may be sent and summed in bfloat16 or wider, within the bound.
A program may use at most 128 MiB of HBM per device.

```python
import math
import jax
import jax.numpy as jnp
from jax import lax

W = 32
HID = 256
NX = 256
MX = 12
KY = 24
KZ = 24
LAYERS = 2
NY = 256
NZ = 16
KMODES = 6912


def block_scale(own_key, shape, shards, smallest, largest):
    def one(axis_at, parts):
        heights = jax.random.uniform(jax.random.fold_in(jax.random.fold_in(own_key, 6), axis_at), (parts,), jnp.float32, smallest / len(shards), largest / len(shards))
        return jnp.repeat(jnp.exp(heights), shape[axis_at] // parts).reshape((-1,) + (1,) * (len(shape) - axis_at - 1))

    gain = one(*shards[0])
    for cut in shards[1:]:
        gain = gain * one(*cut)
    return gain


def gaussian(rng, dims, deviation, bound, shards=(), kind=jnp.bfloat16):
    array = jax.random.normal(rng, dims, jnp.float32) * deviation
    if len(shards) > 0:
        array = block_scale(rng, dims, shards, -0.22, 0.18) * array
    return jnp.clip(array, min=-bound, max=bound).astype(kind)


def setup_inputs(seed: int = 0) -> dict:
    keys = jax.random.split(jax.random.key(seed), 7)
    return {
        "noisy_field": gaussian(keys[0], (W, NZ, NY, NX), 1.0, 6.0, ((1, 8), (2, 4))),
        "spectral_weights": gaussian(keys[1], (LAYERS, 2, KMODES, W, W), (2 * W) ** -0.5, 0.75, ((2, 8), (4, 4))),
        "skip_weights": gaussian(keys[2], (LAYERS, W, W), W ** -0.5, 1.0),
        "in_weights": gaussian(keys[3], (LAYERS, HID, W), W ** -0.5, 1.0),
        "in_bias": gaussian(keys[4], (LAYERS, HID), 0.5, 3.0, (), jnp.float32),
        "out_weights": gaussian(keys[5], (LAYERS, W, HID), HID ** -0.5, 0.375),
    }


def angles(number, positions, length, signed):
    kept = jnp.arange(number, dtype=jnp.int32)
    if signed:
        kept = jnp.where(kept < number // 2, kept, kept - number)
    phases = jnp.mod(kept[:, None] * positions[None, :], length)
    radians = 2.0 * math.pi / length * phases.astype(jnp.float32)
    return (jnp.cos(radians), jnp.sin(radians))

def forward_table(x_positions, length):
    x_cosine, x_sine = angles(MX, x_positions, length, False)
    return jnp.concatenate([x_cosine, -x_sine], 0).T.astype(jnp.bfloat16)

def inverse_table(x_positions, length):
    x_cosine, x_sine = angles(MX, x_positions, length, False)
    factor = jnp.where(jnp.arange(MX) == 0, jnp.float32(1.0), jnp.float32(2.0))
    inverse_scale = 1.0 / math.sqrt(2.0 * KMODES)
    return jnp.concatenate([x_cosine * factor[:, None], -x_sine * factor[:, None]], 0) * inverse_scale

def reference(noisy_field, spectral_weights, skip_weights, in_weights, in_bias, out_weights):
    highest = lax.Precision.HIGHEST
    z_positions = jnp.arange(NZ, dtype=jnp.int32)
    y_positions = jnp.arange(NY, dtype=jnp.int32)
    x_positions = jnp.arange(NX, dtype=jnp.int32)
    z_cosine, z_sine = angles(KZ, z_positions, NZ, True)
    y_cosine, y_sine = angles(KY, y_positions, NY, True)
    table_fwd = forward_table(x_positions, NX)
    table_inv = inverse_table(x_positions, NX)
    forward_scale = 1.0 / math.sqrt(NX * NY * NZ)
    current = noisy_field
    for layer_idx in range(LAYERS):

        def accumulate(running, zindex):
            zplane = lax.dynamic_index_in_dim(current, zindex, 1, keepdims=False)
            xtransform = jnp.dot(zplane.reshape(W * NY, NX), table_fwd, preferred_element_type=jnp.float32).reshape(W, NY, 2, MX)
            along_real = xtransform[:, :, 0]
            along_imag = xtransform[:, :, 1]
            ypass_real = (jnp.einsum('wym,ky->wkm', along_real, y_cosine, precision=highest) + jnp.einsum('wym,ky->wkm', along_imag, y_sine, precision=highest)) * forward_scale
            ypass_imag = (jnp.einsum('wym,ky->wkm', along_imag, y_cosine, precision=highest) - jnp.einsum('wym,ky->wkm', along_real, y_sine, precision=highest)) * forward_scale
            zc_column = lax.dynamic_index_in_dim(z_cosine, zindex, 1, keepdims=False)[None, :, None, None]
            zs_column = lax.dynamic_index_in_dim(z_sine, zindex, 1, keepdims=False)[None, :, None, None]
            sum_real, sum_imag = running
            sum_real = sum_real + ypass_real[:, None] * zc_column + ypass_imag[:, None] * zs_column
            sum_imag = sum_imag + ypass_imag[:, None] * zc_column - ypass_real[:, None] * zs_column
            return ((sum_real, sum_imag), None)
        zeros_init = jnp.zeros((W, KZ, KY, MX), jnp.float32)
        (sum_real, sum_imag), _ = lax.scan(accumulate, (zeros_init, zeros_init), z_positions)
        spec_real = lax.optimization_barrier(sum_real.reshape(W, KMODES).astype(jnp.bfloat16)).astype(jnp.float32)
        spec_imag = lax.optimization_barrier(sum_imag.reshape(W, KMODES).astype(jnp.bfloat16)).astype(jnp.float32)
        coefficients = spectral_weights[layer_idx].astype(jnp.float32)
        modal_real = jnp.einsum('ik,kio->ok', spec_real, coefficients[0], precision=highest) - jnp.einsum('ik,kio->ok', spec_imag, coefficients[1], precision=highest)
        modal_imag = jnp.einsum('ik,kio->ok', spec_real, coefficients[1], precision=highest) + jnp.einsum('ik,kio->ok', spec_imag, coefficients[0], precision=highest)
        modal_real = lax.optimization_barrier(modal_real.astype(jnp.bfloat16)).astype(jnp.float32).reshape(W, KZ, KY * MX)
        modal_imag = lax.optimization_barrier(modal_imag.astype(jnp.bfloat16)).astype(jnp.float32).reshape(W, KZ, KY * MX)
        skip_matrix = skip_weights[layer_idx]
        lift_matrix = in_weights[layer_idx]
        bias_column = in_bias[layer_idx][:, None]
        down_matrix = out_weights[layer_idx]
        layer_input = current

        def plane_output(zindex):
            zc_column = lax.dynamic_index_in_dim(z_cosine, zindex, 1, keepdims=False)
            zs_column = lax.dynamic_index_in_dim(z_sine, zindex, 1, keepdims=False)
            plane_real = jnp.einsum('wkq,k->wq', modal_real, zc_column, precision=highest) - jnp.einsum('wkq,k->wq', modal_imag, zs_column, precision=highest)
            plane_imag = jnp.einsum('wkq,k->wq', modal_real, zs_column, precision=highest) + jnp.einsum('wkq,k->wq', modal_imag, zc_column, precision=highest)
            plane_real = plane_real.reshape(W, KY, MX)
            plane_imag = plane_imag.reshape(W, KY, MX)
            rows_real = jnp.einsum('wkm,ky->wym', plane_real, y_cosine, precision=highest) - jnp.einsum('wkm,ky->wym', plane_imag, y_sine, precision=highest)
            rows_imag = jnp.einsum('wkm,ky->wym', plane_real, y_sine, precision=highest) + jnp.einsum('wkm,ky->wym', plane_imag, y_cosine, precision=highest)
            stacked = jnp.stack([rows_real, rows_imag], axis=2).reshape(W * NY, 2 * MX)
            spatial = jnp.dot(stacked, table_inv, precision=highest).reshape(W, NY * NX)
            zplane = lax.dynamic_index_in_dim(layer_input, zindex, 1, keepdims=False).reshape(W, NY * NX)
            mixed_sum = spatial + jnp.dot(skip_matrix, zplane, preferred_element_type=jnp.float32)
            before = jnp.dot(lift_matrix, mixed_sum.astype(jnp.bfloat16), preferred_element_type=jnp.float32) + bias_column
            hidden = jax.nn.gelu(before, approximate=False).astype(jnp.bfloat16)
            result = mixed_sum + jnp.dot(down_matrix, hidden, preferred_element_type=jnp.float32)
            return result.astype(jnp.bfloat16).reshape(W, NY, NX)
        planes_out = lax.map(plane_output, z_positions)
        current = jnp.moveaxis(planes_out, 0, 1)
    return current
```

```python
import functools
import math

import jax
import jax.numpy as jnp
from jax import lax
from jax.experimental import pallas as pl
from jax.experimental.pallas import tpu as pltpu
from jax.sharding import PartitionSpec as P

MX = 12
KY = 24
KZ = 24
KP = KY // 2
LANES = 128
ROWS = 32
F32 = jnp.float32
BF16 = jnp.bfloat16


def angles(number, positions, length, signed):
    kept = jnp.arange(number, dtype=jnp.int32)
    if signed:
        kept = jnp.where(kept < number // 2, kept, kept - number)
    phases = jnp.mod(kept[:, None] * positions[None, :], length)
    radians = 2.0 * math.pi / length * phases.astype(jnp.float32)
    return (jnp.cos(radians), jnp.sin(radians))


def forward_table(length):
    cosine, sine = angles(MX, jnp.arange(length, dtype=jnp.int32), length, False)
    part = jnp.concatenate([cosine, -sine, -sine, -cosine], 0)
    table = jnp.concatenate([part, part], 0).T.astype(BF16)
    return jnp.pad(table, ((0, 0), (0, LANES - 8 * MX)))


def inverse_table(length):
    cosine, sine = angles(MX, jnp.arange(length, dtype=jnp.int32), length, False)
    factor = jnp.where(jnp.arange(MX) == 0, F32(1.0), F32(2.0))[:, None]
    scale = 1.0 / math.sqrt(2.0 * KZ * KY * MX)
    half = jnp.concatenate([cosine * factor, -sine * factor], 0) * scale
    table = jnp.concatenate([half] * 4, 0).astype(BF16)
    return jnp.pad(table, ((0, LANES - 8 * MX), (0, 0)))


def y_weights(positions, length):
    cosine, sine = angles(KY, positions, length, True)
    both = jnp.stack([cosine, sine], -1).transpose(1, 0, 2)
    lanes = jnp.repeat(both.reshape(positions.shape[0], KP, 4), 2 * MX, axis=2)
    return jnp.pad(lanes, ((0, 0), (0, 0), (0, LANES - 8 * MX)))


def gelu(value):
    return 0.5 * value * (1.0 + lax.erf(value * F32(math.sqrt(0.5))))


def accumulate_modes(along, weight_ref, modes_ref):
    rows, channels = along.shape[0], along.shape[1]

    @pl.when(pl.program_id(1) == 0)
    def _():
        modes_ref[...] = jnp.zeros_like(modes_ref)

    for kp in range(KP):
        total = along[0] * weight_ref[0, kp : kp + 1, :]
        for y in range(1, rows):
            total = total + along[y] * weight_ref[y, kp : kp + 1, :]
        modes_ref[0, kp] += total


def forward_kernel(field_ref, weight_ref, table_ref, modes_ref):
    rows, channels, length = field_ref.shape
    flat = field_ref[...].reshape(rows * channels, length)
    along = jnp.dot(flat, table_ref[...], preferred_element_type=F32)
    accumulate_modes(along.reshape(rows, channels, LANES), weight_ref, modes_ref)


def layer_body(
    field_ref, planes_ref, weight_ref, inverse_ref, skip_ref, lift_ref, bias_ref, down_ref, out_ref
):
    rows, channels, length = field_ref.shape
    parts = []
    for y in range(rows):
        total = planes_ref[0, 0] * weight_ref[y, 0:1, :]
        for kp in range(1, KP):
            total = total + planes_ref[0, kp] * weight_ref[y, kp : kp + 1, :]
        parts.append(total.astype(BF16))
    stacked = jnp.concatenate(parts, 0)
    spatial = jnp.dot(stacked, inverse_ref[...], preferred_element_type=F32)
    wide_spatial = jnp.concatenate(
        [spatial[y * channels : (y + 1) * channels] for y in range(rows)], 1
    )
    wide_field = jnp.concatenate([field_ref[y] for y in range(rows)], 1)
    mixed = wide_spatial + jnp.dot(skip_ref[...], wide_field, preferred_element_type=F32)
    before = jnp.dot(lift_ref[...], mixed.astype(BF16), preferred_element_type=F32)
    hidden = gelu(before + bias_ref[...]).astype(BF16)
    result = mixed + jnp.dot(down_ref[...], hidden, preferred_element_type=F32)
    result = result.astype(BF16)
    for y in range(rows):
        out_ref[y] = result[:, y * length : (y + 1) * length]


def middle_kernel(
    field_ref, planes_ref, weight_ref, inverse_ref, skip_ref, lift_ref, bias_ref, down_ref,
    table_ref, out_ref, modes_ref,
):
    layer_body(
        field_ref, planes_ref, weight_ref, inverse_ref, skip_ref, lift_ref, bias_ref, down_ref,
        out_ref,
    )
    forward_kernel(out_ref, weight_ref, table_ref, modes_ref)


def whole(shape):
    return pl.BlockSpec(shape, lambda z, y: (0,) * len(shape))


def run_forward(field, weights_y, table, planes):
    total, channels, length = field.shape
    steps = total // planes // ROWS
    return pl.pallas_call(
        forward_kernel,
        grid=(planes, steps),
        in_specs=[
            pl.BlockSpec((ROWS, channels, length), lambda z, y: (z * steps + y, 0, 0)),
            pl.BlockSpec((ROWS, KP, LANES), lambda z, y: (y, 0, 0)),
            whole(table.shape),
        ],
        out_specs=pl.BlockSpec((1, KP, channels, LANES), lambda z, y: (z, 0, 0, 0)),
        out_shape=jax.ShapeDtypeStruct((planes, KP, channels, LANES), F32),
        name="forward_modes",
    )(field, weights_y, table)


def run_layer(field, plane_modes, weights_y, inverse, skip, lift, bias, down, table):
    total, channels, length = field.shape
    planes = plane_modes.shape[0]
    steps = total // planes // ROWS
    field_spec = pl.BlockSpec((ROWS, channels, length), lambda z, y: (z * steps + y, 0, 0))
    modes_spec = pl.BlockSpec((1, KP, channels, LANES), lambda z, y: (z, 0, 0, 0))
    field_shape = jax.ShapeDtypeStruct(field.shape, BF16)
    modes_shape = jax.ShapeDtypeStruct(plane_modes.shape, F32)
    args = [field, plane_modes, weights_y, inverse, skip, lift, bias, down]
    specs = [
        field_spec,
        modes_spec,
        pl.BlockSpec((ROWS, KP, LANES), lambda z, y: (y, 0, 0)),
        whole(inverse.shape),
        whole(skip.shape),
        whole(lift.shape),
        whole(bias.shape),
        whole(down.shape),
    ]
    if table is None:
        return pl.pallas_call(
            layer_body,
            grid=(planes, steps),
            in_specs=specs,
            out_specs=field_spec,
            out_shape=field_shape,
            name="last_layer",
        )(*args)
    return pl.pallas_call(
        middle_kernel,
        grid=(planes, steps),
        in_specs=specs + [whole(table.shape)],
        out_specs=[field_spec, modes_spec],
        out_shape=[field_shape, modes_shape],
        name="middle_layer",
    )(*args, table)


def fold_modes(modes, scale):
    planes, _, channels, _ = modes.shape
    split = modes[..., : 8 * MX].reshape(planes, KP, channels, 2, 2, 2, MX)
    folded = (split[:, :, :, :, 0] + split[:, :, :, :, 1]) * scale
    ordered = folded.transpose(0, 4, 2, 1, 3, 5)
    return ordered.reshape(planes * 2, channels, KY * MX)


def unfold_modes(rows, planes):
    channels = rows.shape[1]
    real, imag = (
        rows.astype(F32).reshape(planes, 2, channels, KP, 2, MX)[:, part] for part in range(2)
    )
    lanes = jnp.stack([real, imag, -imag, real], axis=4)
    lanes = lanes.transpose(0, 2, 1, 3, 4, 5).reshape(planes, KP, channels, 8 * MX)
    return jnp.pad(lanes, ((0, 0), (0, 0), (0, 0), (0, LANES - 8 * MX)))


def greet(axis, count):
    me = lax.axis_index(axis)
    barrier = pltpu.get_barrier_semaphore()
    for step in range(1, count):
        pl.semaphore_signal(
            barrier,
            inc=1,
            device_id={axis: lax.rem(me + step, count)},
            device_id_type=pl.DeviceIdType.MESH,
        )
    pl.semaphore_wait(barrier, count - 1)
    return me


def gather_kernel(axis, count, own_ref, out_ref, held, send_sem, recv_sem):
    me = greet(axis, count)
    copies = []
    for step in range(1, count):
        copy = pltpu.make_async_remote_copy(
            src_ref=own_ref,
            dst_ref=held.at[step],
            send_sem=send_sem.at[step],
            recv_sem=recv_sem.at[step],
            device_id={axis: lax.rem(me + step, count)},
            device_id_type=pl.DeviceIdType.MESH,
        )
        copy.start()
        copies.append(copy)
    out_ref[me] = own_ref[...]
    for step, copy in enumerate(copies, 1):
        copy.wait_recv()
        out_ref[lax.rem(me - step + count, count)] = held[step]
    for copy in copies:
        copy.wait_send()


def scatter_kernel(axis, count, own_ref, out_ref, held, send_sem, recv_sem):
    me = greet(axis, count)
    copies = []
    for step in range(1, count):
        peer = lax.rem(me + step, count)
        copy = pltpu.make_async_remote_copy(
            src_ref=own_ref.at[peer],
            dst_ref=held.at[step],
            send_sem=send_sem.at[step],
            recv_sem=recv_sem.at[step],
            device_id={axis: peer},
            device_id_type=pl.DeviceIdType.MESH,
        )
        copy.start()
        copies.append(copy)
    total = own_ref[me].astype(F32)
    for step, copy in enumerate(copies, 1):
        copy.wait_recv()
        total = total + held[step].astype(F32)
    out_ref[...] = total.astype(out_ref.dtype)
    for copy in copies:
        copy.wait_send()


def communicate(kernel, value, axis, block, out_shape, out_type, number):
    count = lax.axis_size(axis)
    return pl.pallas_call(
        functools.partial(kernel, axis, count),
        out_shape=jax.ShapeDtypeStruct(out_shape, out_type),
        in_specs=[pl.BlockSpec(memory_space=pltpu.VMEM)],
        out_specs=pl.BlockSpec(memory_space=pltpu.VMEM),
        scratch_shapes=[
            pltpu.VMEM((count,) + block, value.dtype),
            pltpu.SemaphoreType.DMA((count,)),
            pltpu.SemaphoreType.DMA((count,)),
        ],
        compiler_params=pltpu.CompilerParams(collective_id=number, has_side_effects=True),
        name="exchange_" + axis,
    )(value)


def gather(value, axis, number):
    count = lax.axis_size(axis)
    return communicate(
        gather_kernel, value, axis, value.shape, (count,) + value.shape, value.dtype, number
    )


def scatter_sum(value, axis, out_type, number):
    return communicate(
        scatter_kernel, value, axis, value.shape[1:], value.shape[1:], out_type, number
    )


def z_matrix(cosine, sine, inverse):
    sign = -1.0 if inverse else 1.0
    return jnp.stack(
        [jnp.stack([cosine, sign * sine]), jnp.stack([-sign * sine, cosine])]
    )


def weigh(spectrum, coefficients):
    real, imag = spectrum[0], spectrum[1]

    def product(left, right):
        return jnp.einsum("zcq,zqco->zoq", left, right, preferred_element_type=F32)

    modal_real = product(real, coefficients[0]) - product(imag, coefficients[1])
    modal_imag = product(real, coefficients[1]) + product(imag, coefficients[0])
    return jnp.stack([modal_real, modal_imag]).astype(BF16)


def exchange(partial, local_weights, planes, full_z, number):
    highest = lax.Precision.HIGHEST
    channels = partial.shape[1]
    modes = KY * MX
    here_z = lax.axis_index("gz") * planes + jnp.arange(planes, dtype=jnp.int32)
    all_z = jnp.arange(full_z, dtype=jnp.int32)
    own_modes = local_weights.shape[1]
    groups = lax.axis_size("gz")
    if own_modes % modes == 0:
        own_kz = own_modes // modes
        cosine, sine = angles(KZ, all_z, full_z, True)
        first = lax.axis_index("gz") * own_kz
        cosine = lax.dynamic_slice_in_dim(cosine, first, own_kz, 0)
        sine = lax.dynamic_slice_in_dim(sine, first, own_kz, 0)
        forward = z_matrix(cosine, sine, False).transpose(0, 2, 3, 1)
        forward = forward.reshape(2 * own_kz, 2 * full_z)
        quarters = lax.axis_size("gy")
        share = channels // quarters
        split = partial.reshape(planes * 2, quarters, share, modes).transpose(1, 0, 2, 3)
        summed = scatter_sum(
            split.reshape(quarters, planes * 2 * share, modes), "gy", BF16, number
        )
        gathered = gather(summed, "gz", number + 1)
        spectrum = jnp.dot(
            forward,
            gathered.reshape(2 * full_z, share * modes).astype(F32),
            precision=highest,
        ).astype(BF16)
        spectrum = gather(spectrum.reshape(2 * own_kz * share, modes), "gy", number + 2)
        spectrum = spectrum.reshape(quarters, 2, own_kz, share, modes).transpose(1, 2, 0, 3, 4)
        spectrum = spectrum.reshape(2, own_kz, channels, modes)
        coefficients = local_weights.reshape(2, own_kz, modes, channels, -1)
        modal = weigh(spectrum, coefficients)
        outputs = modal.shape[2]
        modal = gather(modal.reshape(2 * own_kz * outputs, modes), "gz", number + 3)
        modal = modal.reshape(groups * 2 * own_kz, outputs * modes)
        cosine, sine = angles(KZ, here_z, full_z, True)
        inverse = z_matrix(cosine, sine, True).reshape(2, 2, groups, own_kz, planes)
        inverse = inverse.transpose(4, 0, 2, 1, 3).reshape(planes * 2, groups * 2 * own_kz)
        rows = jnp.dot(inverse, modal.astype(F32), precision=highest)
        rows = gather(
            rows.astype(BF16).reshape(planes * 2 * outputs, modes), "gy", number + 4
        )
        rows = rows.reshape(quarters, planes * 2, outputs, modes).transpose(1, 0, 2, 3)
        return rows.reshape(planes * 2, channels, modes)
    cosine, sine = angles(KZ, here_z, full_z, True)
    forward = z_matrix(cosine, sine, False).transpose(0, 2, 3, 1)
    sums = jnp.einsum(
        "akr,rcq->ackq", forward.reshape(2, KZ, planes * 2), partial, precision=highest
    ).reshape(2, channels, KZ * modes)
    sums = lax.psum_scatter(sums, "gz", scatter_dimension=2, tiled=True)
    spectrum = lax.psum(sums, "gy").astype(BF16)[:, None]
    coefficients = lax.all_gather(local_weights, "gy", axis=3, tiled=True)[:, None]
    modal = weigh(spectrum, coefficients)[:, 0]
    modal = lax.all_gather(modal, "gz", axis=2, tiled=True)
    modal = modal.astype(F32).reshape(2, channels, KZ, modes)
    inverse = z_matrix(cosine, sine, True)
    rows = jnp.einsum("abkz,bckq->zacq", inverse, modal, precision=highest)
    return rows.reshape(planes * 2, channels, modes)


def per_device(noisy_field, spectral_weights, skip_weights, in_weights, in_bias, out_weights):
    channels, planes, quarter, length_x = noisy_field.shape
    layer_count = spectral_weights.shape[0]
    full_y = quarter * lax.axis_size("gy")
    full_z = planes * lax.axis_size("gz")
    y_positions = lax.axis_index("gy") * quarter + jnp.arange(quarter, dtype=jnp.int32)
    weights_y = y_weights(y_positions, full_y)
    table = forward_table(length_x)
    inverse = inverse_table(length_x)
    scale = 1.0 / math.sqrt(length_x * full_y * full_z)
    field = noisy_field.transpose(1, 2, 0, 3).reshape(planes * quarter, channels, length_x)
    modes = run_forward(field, weights_y, table, planes)
    for layer in range(layer_count):
        rows = exchange(
            fold_modes(modes, scale), spectral_weights[layer], planes, full_z, 5 * layer
        )
        last = layer == layer_count - 1
        result = run_layer(
            field,
            unfold_modes(rows, planes),
            weights_y,
            inverse,
            skip_weights[layer],
            in_weights[layer],
            in_bias[layer][:, None],
            out_weights[layer],
            None if last else table,
        )
        if last:
            field = result
        else:
            field, modes = result
    return field.reshape(planes, quarter, channels, length_x).transpose(2, 0, 1, 3)


def solution(mesh):
    in_specs = (P(None, "gz", "gy", None), P(None, None, "gz", None, "gy"), P(), P(), P(), P())
    out_specs = P(None, "gz", "gy", None)
    return jax.shard_map(
        per_device, mesh=mesh, in_specs=in_specs, out_specs=out_specs, check_vma=False
    )
```

```python
import functools
import math

import jax
import jax.numpy as jnp
from jax import lax
from jax.experimental import pallas as pl
from jax.experimental.pallas import tpu as pltpu
from jax.sharding import PartitionSpec as P

MX = 12
KY = 24
KZ = 24
KP = KY // 2
LANES = 128
ROWS = 32
F32 = jnp.float32
BF16 = jnp.bfloat16


def angles(number, positions, length, signed):
    kept = jnp.arange(number, dtype=jnp.int32)
    if signed:
        kept = jnp.where(kept < number // 2, kept, kept - number)
    phases = jnp.mod(kept[:, None] * positions[None, :], length)
    radians = 2.0 * math.pi / length * phases.astype(jnp.float32)
    return (jnp.cos(radians), jnp.sin(radians))


def forward_table(length):
    cosine, sine = angles(MX, jnp.arange(length, dtype=jnp.int32), length, False)
    part = jnp.concatenate([cosine, -sine, -sine, -cosine], 0)
    table = jnp.concatenate([part, part], 0).T.astype(BF16)
    return jnp.pad(table, ((0, 0), (0, LANES - 8 * MX)))


def inverse_table(length):
    cosine, sine = angles(MX, jnp.arange(length, dtype=jnp.int32), length, False)
    factor = jnp.where(jnp.arange(MX) == 0, F32(1.0), F32(2.0))[:, None]
    scale = 1.0 / math.sqrt(2.0 * KZ * KY * MX)
    half = jnp.concatenate([cosine * factor, -sine * factor], 0) * scale
    table = jnp.concatenate([half] * 4, 0).astype(BF16)
    return jnp.pad(table, ((0, LANES - 8 * MX), (0, 0)))


def y_weights(positions, length):
    cosine, sine = angles(KY, positions, length, True)
    both = jnp.stack([cosine, sine], -1).transpose(1, 0, 2)
    lanes = jnp.repeat(both.reshape(positions.shape[0], KP, 4), 2 * MX, axis=2)
    return jnp.pad(lanes, ((0, 0), (0, 0), (0, LANES - 8 * MX)))


def gelu(value):
    return 0.5 * value * (1.0 + lax.erf(value * F32(math.sqrt(0.5))))


def accumulate_modes(along, weight_ref, modes_ref):
    rows, channels = along.shape[0], along.shape[1]

    @pl.when(pl.program_id(1) == 0)
    def _():
        modes_ref[...] = jnp.zeros_like(modes_ref)

    for kp in range(KP):
        total = along[0] * weight_ref[0, kp : kp + 1, :]
        for y in range(1, rows):
            total = total + along[y] * weight_ref[y, kp : kp + 1, :]
        modes_ref[0, kp] += total


def forward_kernel(field_ref, weight_ref, table_ref, modes_ref):
    rows, channels, length = field_ref.shape
    flat = field_ref[...].reshape(rows * channels, length)
    along = jnp.dot(flat, table_ref[...], preferred_element_type=F32)
    accumulate_modes(along.reshape(rows, channels, LANES), weight_ref, modes_ref)


def layer_body(
    field_ref, planes_ref, weight_ref, inverse_ref, skip_ref, lift_ref, bias_ref, down_ref, out_ref
):
    rows, channels, length = field_ref.shape
    parts = []
    for y in range(rows):
        total = planes_ref[0, 0] * weight_ref[y, 0:1, :]
        for kp in range(1, KP):
            total = total + planes_ref[0, kp] * weight_ref[y, kp : kp + 1, :]
        parts.append(total.astype(BF16))
    stacked = jnp.concatenate(parts, 0)
    spatial = jnp.dot(stacked, inverse_ref[...], preferred_element_type=F32)
    wide_spatial = jnp.concatenate(
        [spatial[y * channels : (y + 1) * channels] for y in range(rows)], 1
    )
    wide_field = jnp.concatenate([field_ref[y] for y in range(rows)], 1)
    mixed = wide_spatial + jnp.dot(skip_ref[...], wide_field, preferred_element_type=F32)
    before = jnp.dot(lift_ref[...], mixed.astype(BF16), preferred_element_type=F32)
    hidden = gelu(before + bias_ref[...]).astype(BF16)
    result = mixed + jnp.dot(down_ref[...], hidden, preferred_element_type=F32)
    result = result.astype(BF16)
    for y in range(rows):
        out_ref[y] = result[:, y * length : (y + 1) * length]


def middle_kernel(
    field_ref, planes_ref, weight_ref, inverse_ref, skip_ref, lift_ref, bias_ref, down_ref,
    table_ref, out_ref, modes_ref,
):
    layer_body(
        field_ref, planes_ref, weight_ref, inverse_ref, skip_ref, lift_ref, bias_ref, down_ref,
        out_ref,
    )
    forward_kernel(out_ref, weight_ref, table_ref, modes_ref)


def whole(shape):
    return pl.BlockSpec(shape, lambda z, y: (0,) * len(shape))


def run_forward(field, weights_y, table, planes):
    total, channels, length = field.shape
    steps = total // planes // ROWS
    return pl.pallas_call(
        forward_kernel,
        grid=(planes, steps),
        in_specs=[
            pl.BlockSpec((ROWS, channels, length), lambda z, y: (z * steps + y, 0, 0)),
            pl.BlockSpec((ROWS, KP, LANES), lambda z, y: (y, 0, 0)),
            whole(table.shape),
        ],
        out_specs=pl.BlockSpec((1, KP, channels, LANES), lambda z, y: (z, 0, 0, 0)),
        out_shape=jax.ShapeDtypeStruct((planes, KP, channels, LANES), F32),
        name="forward_modes",
    )(field, weights_y, table)


def run_layer(field, plane_modes, weights_y, inverse, skip, lift, bias, down, table):
    total, channels, length = field.shape
    planes = plane_modes.shape[0]
    steps = total // planes // ROWS
    field_spec = pl.BlockSpec((ROWS, channels, length), lambda z, y: (z * steps + y, 0, 0))
    modes_spec = pl.BlockSpec((1, KP, channels, LANES), lambda z, y: (z, 0, 0, 0))
    field_shape = jax.ShapeDtypeStruct(field.shape, BF16)
    modes_shape = jax.ShapeDtypeStruct(plane_modes.shape, F32)
    args = [field, plane_modes, weights_y, inverse, skip, lift, bias, down]
    specs = [
        field_spec,
        modes_spec,
        pl.BlockSpec((ROWS, KP, LANES), lambda z, y: (y, 0, 0)),
        whole(inverse.shape),
        whole(skip.shape),
        whole(lift.shape),
        whole(bias.shape),
        whole(down.shape),
    ]
    if table is None:
        return pl.pallas_call(
            layer_body,
            grid=(planes, steps),
            in_specs=specs,
            out_specs=field_spec,
            out_shape=field_shape,
            name="last_layer",
        )(*args)
    return pl.pallas_call(
        middle_kernel,
        grid=(planes, steps),
        in_specs=specs + [whole(table.shape)],
        out_specs=[field_spec, modes_spec],
        out_shape=[field_shape, modes_shape],
        name="middle_layer",
    )(*args, table)


def fold_modes(modes, scale):
    planes, _, channels, _ = modes.shape
    split = modes[..., : 8 * MX].reshape(planes, KP, channels, 2, 2, 2, MX)
    folded = (split[:, :, :, :, 0] + split[:, :, :, :, 1]) * scale
    ordered = folded.transpose(0, 4, 2, 1, 3, 5)
    return ordered.reshape(planes * 2, channels, KY * MX)


def unfold_modes(rows, planes):
    channels = rows.shape[1]
    real, imag = (
        rows.astype(F32).reshape(planes, 2, channels, KP, 2, MX)[:, part] for part in range(2)
    )
    lanes = jnp.stack([real, imag, -imag, real], axis=4)
    lanes = lanes.transpose(0, 2, 1, 3, 4, 5).reshape(planes, KP, channels, 8 * MX)
    return jnp.pad(lanes, ((0, 0), (0, 0), (0, 0), (0, LANES - 8 * MX)))


def greet(axes):
    barrier = pltpu.get_barrier_semaphore()
    total = 0
    for axis, count in axes:
        me = lax.axis_index(axis)
        for step in range(1, count):
            pl.semaphore_signal(
                barrier,
                inc=1,
                device_id={axis: lax.rem(me + step, count)},
                device_id_type=pl.DeviceIdType.MESH,
            )
        total += count - 1
    pl.semaphore_wait(barrier, total)


def spread(axis, count, source, held, send_sem, recv_sem):
    me = lax.axis_index(axis)
    copies = []
    for step in range(1, count):
        peer = lax.rem(me + step, count)
        copy = pltpu.make_async_remote_copy(
            src_ref=source(peer),
            dst_ref=held.at[step],
            send_sem=send_sem.at[step],
            recv_sem=recv_sem.at[step],
            device_id={axis: peer},
            device_id_type=pl.DeviceIdType.MESH,
        )
        copy.start()
        copies.append(copy)
    return copies


def collect(axis, count, own, held, copies, out_ref):
    me = lax.axis_index(axis)
    out_ref[me] = own
    for step, copy in enumerate(copies, 1):
        copy.wait_recv()
        out_ref[lax.rem(me - step + count, count)] = held[step]


def z_and_y(groups, quarters, own_ref, matrix_ref, out_ref, held_z, all_z, stage, held_y, sems):
    send_z, recv_z, send_y, recv_y = sems
    first = spread("gz", groups, lambda peer: own_ref, held_z, send_z, recv_z)
    collect("gz", groups, own_ref[...], held_z, first, all_z)
    rows = all_z[...].reshape(-1, all_z.shape[-1]).astype(F32)
    stage[...] = jnp.dot(
        matrix_ref[...], rows, precision=lax.Precision.HIGHEST, preferred_element_type=F32
    ).astype(BF16)
    second = spread("gy", quarters, lambda peer: stage, held_y, send_y, recv_y)
    collect("gy", quarters, stage[...], held_y, second, out_ref)
    return first + second


def sum_kernel(
    groups, quarters, own_ref, matrix_ref, out_ref, held_sum, summed, held_z, all_z, stage, held_y,
    send_sum, recv_sum, *sems,
):
    greet((("gz", groups), ("gy", quarters)))
    copies = spread("gy", quarters, lambda peer: own_ref.at[peer], held_sum, send_sum, recv_sum)
    total = own_ref[lax.axis_index("gy")]
    for step, copy in enumerate(copies, 1):
        copy.wait_recv()
        total = total + held_sum[step]
    summed[...] = total.astype(BF16)
    copies += z_and_y(
        groups, quarters, summed, matrix_ref, out_ref, held_z, all_z, stage, held_y, sems
    )
    for copy in copies:
        copy.wait_send()


def spread_kernel(
    groups, quarters, own_ref, matrix_ref, out_ref, held_z, all_z, stage, held_y, *sems
):
    greet((("gz", groups), ("gy", quarters)))
    copies = z_and_y(
        groups, quarters, own_ref, matrix_ref, out_ref, held_z, all_z, stage, held_y, sems
    )
    for copy in copies:
        copy.wait_send()


def communicate(value, matrix, summing, number):
    groups, quarters = lax.axis_size("gz"), lax.axis_size("gy")
    block = value.shape[-2:]
    result = (matrix.shape[0], block[1])
    vmem = pl.BlockSpec(memory_space=pltpu.VMEM)
    scratch = [
        pltpu.VMEM((groups,) + block, BF16),
        pltpu.VMEM((groups,) + block, BF16),
        pltpu.VMEM(result, BF16),
        pltpu.VMEM((quarters,) + result, BF16),
    ]
    sems = [pltpu.SemaphoreType.DMA((count,)) for count in (groups, groups, quarters, quarters)]
    if summing:
        scratch = [pltpu.VMEM((quarters,) + block, F32), pltpu.VMEM(block, BF16)] + scratch
        sems = [pltpu.SemaphoreType.DMA((quarters,))] * 2 + sems
    return pl.pallas_call(
        functools.partial(sum_kernel if summing else spread_kernel, groups, quarters),
        out_shape=jax.ShapeDtypeStruct((quarters,) + result, BF16),
        in_specs=[vmem, vmem],
        out_specs=vmem,
        scratch_shapes=scratch + sems,
        compiler_params=pltpu.CompilerParams(collective_id=number, has_side_effects=True),
        name="exchange",
    )(value, matrix)


def z_matrix(cosine, sine, inverse):
    sign = -1.0 if inverse else 1.0
    return jnp.stack(
        [jnp.stack([cosine, sign * sine]), jnp.stack([-sign * sine, cosine])]
    )


def weigh(spectrum, coefficients):
    real, imag = spectrum[0], spectrum[1]

    def product(left, right):
        return jnp.einsum("zcq,zqco->zoq", left, right, preferred_element_type=F32)

    modal_real = product(real, coefficients[0]) - product(imag, coefficients[1])
    modal_imag = product(real, coefficients[1]) + product(imag, coefficients[0])
    return jnp.stack([modal_real, modal_imag]).astype(BF16)


def exchange(partial, local_weights, planes, full_z, number):
    highest = lax.Precision.HIGHEST
    channels = partial.shape[1]
    modes = KY * MX
    here_z = lax.axis_index("gz") * planes + jnp.arange(planes, dtype=jnp.int32)
    all_z = jnp.arange(full_z, dtype=jnp.int32)
    own_modes = local_weights.shape[1]
    groups = lax.axis_size("gz")
    if own_modes % modes == 0:
        own_kz = own_modes // modes
        cosine, sine = angles(KZ, all_z, full_z, True)
        first = lax.axis_index("gz") * own_kz
        cosine = lax.dynamic_slice_in_dim(cosine, first, own_kz, 0)
        sine = lax.dynamic_slice_in_dim(sine, first, own_kz, 0)
        forward = z_matrix(cosine, sine, False).transpose(0, 2, 3, 1)
        forward = forward.reshape(2 * own_kz, 2 * full_z)
        quarters = lax.axis_size("gy")
        share = channels // quarters
        split = partial.reshape(planes * 2, quarters, share, modes).transpose(1, 0, 2, 3)
        spectrum = communicate(
            split.reshape(quarters, planes * 2 * share, modes),
            jnp.kron(forward, jnp.eye(share, dtype=F32)),
            True,
            number,
        )
        spectrum = spectrum.reshape(quarters, 2, own_kz, share, modes).transpose(1, 2, 0, 3, 4)
        spectrum = spectrum.reshape(2, own_kz, channels, modes)
        coefficients = local_weights.reshape(2, own_kz, modes, channels, -1)
        modal = weigh(spectrum, coefficients)
        outputs = modal.shape[2]
        cosine, sine = angles(KZ, here_z, full_z, True)
        inverse = z_matrix(cosine, sine, True).reshape(2, 2, groups, own_kz, planes)
        inverse = inverse.transpose(4, 0, 2, 1, 3).reshape(planes * 2, groups * 2 * own_kz)
        rows = communicate(
            modal.reshape(2 * own_kz * outputs, modes),
            jnp.kron(inverse, jnp.eye(outputs, dtype=F32)),
            False,
            number + 1,
        )
        rows = rows.reshape(quarters, planes * 2, outputs, modes).transpose(1, 0, 2, 3)
        return rows.reshape(planes * 2, channels, modes)
    cosine, sine = angles(KZ, here_z, full_z, True)
    forward = z_matrix(cosine, sine, False).transpose(0, 2, 3, 1)
    sums = jnp.einsum(
        "akr,rcq->ackq", forward.reshape(2, KZ, planes * 2), partial, precision=highest
    ).reshape(2, channels, KZ * modes)
    sums = lax.psum_scatter(sums, "gz", scatter_dimension=2, tiled=True)
    spectrum = lax.psum(sums, "gy").astype(BF16)[:, None]
    coefficients = lax.all_gather(local_weights, "gy", axis=3, tiled=True)[:, None]
    modal = weigh(spectrum, coefficients)[:, 0]
    modal = lax.all_gather(modal, "gz", axis=2, tiled=True)
    modal = modal.astype(F32).reshape(2, channels, KZ, modes)
    inverse = z_matrix(cosine, sine, True)
    rows = jnp.einsum("abkz,bckq->zacq", inverse, modal, precision=highest)
    return rows.reshape(planes * 2, channels, modes)


def per_device(noisy_field, spectral_weights, skip_weights, in_weights, in_bias, out_weights):
    channels, planes, quarter, length_x = noisy_field.shape
    layer_count = spectral_weights.shape[0]
    full_y = quarter * lax.axis_size("gy")
    full_z = planes * lax.axis_size("gz")
    y_positions = lax.axis_index("gy") * quarter + jnp.arange(quarter, dtype=jnp.int32)
    weights_y = y_weights(y_positions, full_y)
    table = forward_table(length_x)
    inverse = inverse_table(length_x)
    scale = 1.0 / math.sqrt(length_x * full_y * full_z)
    field = noisy_field.transpose(1, 2, 0, 3).reshape(planes * quarter, channels, length_x)
    modes = run_forward(field, weights_y, table, planes)
    for layer in range(layer_count):
        rows = exchange(
            fold_modes(modes, scale), spectral_weights[layer], planes, full_z, 2 * layer
        )
        last = layer == layer_count - 1
        result = run_layer(
            field,
            unfold_modes(rows, planes),
            weights_y,
            inverse,
            skip_weights[layer],
            in_weights[layer],
            in_bias[layer][:, None],
            out_weights[layer],
            None if last else table,
        )
        if last:
            field = result
        else:
            field, modes = result
    return field.reshape(planes, quarter, channels, length_x).transpose(2, 0, 1, 3)


def solution(mesh):
    in_specs = (P(None, "gz", "gy", None), P(None, None, "gz", None, "gy"), P(), P(), P(), P())
    out_specs = P(None, "gz", "gy", None)
    return jax.shard_map(
        per_device, mesh=mesh, in_specs=in_specs, out_specs=out_specs, check_vma=False
    )
```
